32 devices in a mesh: tiles: 2 (over x), rows: 16 (over z, y, core).
Axes of the slice: x: 2, y: 2, z: 4, core: 2. Of those that a mesh axis runs over, the one named last changes fastest.
Arguments:
- reflect: bfloat16 [128, 6, 32, 2048], P('rows', None, None, 'tiles'), parts along dimension 3, may hold values from 0 to 6.5
- clear_conf: int32 [128, 32, 2048], P('rows', None, 'tiles'), parts along dimension 2, may hold values from 0 to 100
- sun_view: int32 [128, 3, 32, 2048], P('rows', None, None, 'tiles'), parts along dimension 3, may hold values from 0 to 18000, as said below
- sensor_id: int32 [128], replicated, may hold values from 0 to 3
- band_gain: float32 [4, 6], replicated, may hold values from 0.5 to 1.5
- sensor_weight: float32 [4], replicated, may hold values from 0.5 to 2
- prior: float32 [32, 18, 2048], P('rows', None, 'tiles'), parts along dimension 2, may hold values from -1.75 to 1.75
Outputs:
- brdf_weights: float32 [32, 18, 2048], P('rows', None, 'tiles'), parts along dimension 2
The draws below stay inside these ranges and needn't reach their ends.
There are 2 independent parts, one for each index of `tiles`. The reference program is written for one: setup_inputs(seed, part) draws one part's arguments, and reference() takes and returns one part's arrays. A program takes and returns all parts, laid end to end along the dimension named above; an argument that names none is the same for every part. Nothing has to cross between parts.
Inputs may be any that keep to these rules, and one draw needn't show every extreme that they name: `sun_view`: component 0 is the solar zenith, 2000 to 7000; component 1 the view zenith, 0 to 1500; component 2 the relative azimuth, 0 to 18000.
All inputs are finite; a program needn't handle non-finite values.
Results may differ from the reference program's by a relative error of at most 0.0003.
Values may be sent and summed in bfloat16 or wider, within the bound.
A program may use at most 128 MiB of HBM per device.

```python
import math
import jax
import jax.numpy as jnp
from jax import lax

DATES = 128
BANDS = 6
SENSORS = 4
COLS = 1024
ITERS = 3
COEFS = 18
ROWS_TOTAL = 32


def draw_reflect(key, part):
    key_albedo = jax.random.fold_in(key, 11)
    key_rough = jax.random.fold_in(key, 12)
    position = jnp.arange(ROWS_TOTAL, dtype=jnp.float32) / max(ROWS_TOTAL - 1, 1)
    rise = 3.0
    rough = jax.random.uniform(key_rough, (DATES, BANDS, ROWS_TOTAL, COLS), jnp.float32, 0.7, 1.3)
    gradient = jnp.exp(math.log(rise) * position)[None, None, :, None]
    albedo = jnp.exp(jax.random.uniform(key_albedo, (1, BANDS, ROWS_TOTAL, COLS), jnp.float32, math.log(0.05), math.log(0.5)))
    return (gradient * albedo * rough).astype(jnp.bfloat16)


def draw_sun_view(key, part):
    grid_shape = (DATES, 1, ROWS_TOTAL, COLS)
    sun_zen = jax.random.randint(jax.random.fold_in(key, 21), grid_shape, 2000, 7001, dtype=jnp.int32)
    view_zen = jax.random.randint(jax.random.fold_in(key, 22), grid_shape, 0, 1501, dtype=jnp.int32)
    azimuth = jax.random.randint(jax.random.fold_in(key, 23), grid_shape, 0, 18001, dtype=jnp.int32)
    return jnp.concatenate([sun_zen, view_zen, azimuth], axis=1)


def place_ends(values, rng, low, high):
    longest = values.shape.index(max(values.shape))
    spots = []
    for shift in (0, 1):
        where = [jax.random.randint(jax.random.fold_in(rng, axis), (), 0, length) for axis, length in enumerate(values.shape)]
        where[longest] = (where[longest] + shift) % values.shape[longest]
        spots.append(tuple(where))
    return values.at[spots[0]].set(low).at[spots[1]].set(high)


def shard_levels(stream_key, shape, shards, least, high):
    factor_of = 1.0
    for axis_at, blocks in shards:
        heights = jax.random.uniform(jax.random.fold_in(jax.random.fold_in(stream_key, 6), axis_at), (blocks,), jnp.float32, least / len(shards), high / len(shards))
        factor_of = factor_of * jnp.repeat(jnp.exp(heights), shape[axis_at] // blocks).reshape((-1,) + (1,) * (len(shape) - 1 - axis_at))
    return factor_of


def scatter_about(key, extent, scale, bound, pieces=(), kind=jnp.bfloat16):
    values = jax.random.normal(key, extent, jnp.float32) * scale
    if len(pieces) > 0:
        values = shard_levels(key, extent, pieces, -0.22, 0.18) * values
    return jnp.clip(values, min=-bound, max=bound).astype(kind)


def setup_inputs(seed: int = 0, part: int = 0) -> dict:
    seeds = jax.random.split(jax.random.key(seed), 8)
    part_keys = jax.random.split(jax.random.fold_in(seeds[7], part), 8)
    return {
        "reflect": draw_reflect(jax.random.fold_in(jax.random.fold_in(seeds[7], part), 71), part),
        "clear_conf": place_ends(jax.random.randint(part_keys[1], (DATES, ROWS_TOTAL, COLS), 0, 101), jax.random.fold_in(part_keys[1], 1), 0, 100).astype(jnp.int32),
        "sun_view": draw_sun_view(jax.random.fold_in(jax.random.fold_in(seeds[7], part), 71), part),
        "sensor_id": place_ends(jax.random.randint(seeds[3], (DATES,), 0, SENSORS), jax.random.fold_in(seeds[3], 1), 0, SENSORS - 1).astype(jnp.int32),
        "band_gain": jnp.clip(1.0 + 0.1 * jax.random.normal(seeds[4], (SENSORS, BANDS), jnp.float32), 0.5, 1.5),
        "sensor_weight": jnp.clip(jnp.exp(jax.random.uniform(seeds[5], (SENSORS,), jnp.float32, math.log(0.5), math.log(2.0))), 0.5, 2.0),
        "prior": scatter_about(part_keys[6], (ROWS_TOTAL, COEFS, COLS), 0.3, 1.75, ((0, 16),), jnp.float32),
    }


to_radian = math.pi / 18000.0
prior_pull = 0.1
smooth_pull = 0.5

def ross_li(sun_view):
    solar_zen = sun_view[:, 0].astype(jnp.float32) * to_radian
    view_zen = sun_view[:, 1].astype(jnp.float32) * to_radian
    azimuth = sun_view[:, 2].astype(jnp.float32) * to_radian
    cos_sun, sin_sun = (jnp.cos(solar_zen), jnp.sin(solar_zen))
    cos_view, sin_view = (jnp.cos(view_zen), jnp.sin(view_zen))
    cos_azim, sin_azim = (jnp.cos(azimuth), jnp.sin(azimuth))
    cos_phase = cos_sun * cos_view + sin_sun * sin_view * cos_azim
    phase_angle = jnp.arccos(cos_phase)
    volume = ((0.5 * math.pi - phase_angle) * cos_phase + jnp.sin(phase_angle)) / (cos_sun + cos_view) - 0.25 * math.pi
    tan_sun = sin_sun / cos_sun
    tan_view = sin_view / cos_view
    sec_sun = 1.0 / cos_sun
    sec_view = 1.0 / cos_view
    spread = tan_sun * tan_sun + tan_view * tan_view - 2.0 * tan_sun * tan_view * cos_azim
    cross_term = tan_sun * tan_view * sin_azim
    cos_correlation = jnp.minimum(2.0 * jnp.sqrt(spread + cross_term * cross_term) / (sec_sun + sec_view), 1.0)
    correlation_angle = jnp.arccos(cos_correlation)
    correlation = (correlation_angle - jnp.sin(correlation_angle) * cos_correlation) * (sec_sun + sec_view) / math.pi
    geometric = correlation - sec_sun - sec_view + 0.5 * (1.0 + cos_phase) * sec_sun * sec_view
    return (volume, geometric)

def normal_terms(reflect, clear_conf, sun_view, date_gain, date_weight):
    volume, geometric = ross_li(sun_view)
    weight = date_weight[:, None, None] * clear_conf.astype(jnp.float32) * 0.01
    weighted_vol = weight * volume
    weighted_geo = weight * geometric
    entries = [lax.optimization_barrier(jnp.sum(weight, 0)), lax.optimization_barrier(jnp.sum(weighted_vol, 0)), lax.optimization_barrier(jnp.sum(weighted_geo, 0)), lax.optimization_barrier(jnp.sum(weighted_vol * volume, 0)), lax.optimization_barrier(jnp.sum(weighted_vol * geometric, 0)), lax.optimization_barrier(jnp.sum(weighted_geo * geometric, 0))]
    signal = reflect.astype(jnp.float32) * date_gain[:, :, None, None]
    for band_index in range(signal.shape[1]):
        band_signal = signal[:, band_index]
        entries = entries + [lax.optimization_barrier(jnp.sum(weight * band_signal, 0)), lax.optimization_barrier(jnp.sum(weighted_vol * band_signal, 0)), lax.optimization_barrier(jnp.sum(weighted_geo * band_signal, 0))]
    return jnp.stack(entries, axis=1)

def couple(field, normal):
    row_count, coef_count, col_count = field.shape
    grouped = field.reshape(row_count, coef_count // 3, 3, col_count)
    iso_coef, vol_coef, geo_coef = (grouped[:, :, 0], grouped[:, :, 1], grouped[:, :, 2])
    entry = [normal[:, index_n:index_n + 1] for index_n in range(6)]
    result = jnp.stack([entry[0] * iso_coef + entry[1] * vol_coef + entry[2] * geo_coef, entry[1] * iso_coef + entry[3] * vol_coef + entry[4] * geo_coef, entry[2] * iso_coef + entry[4] * vol_coef + entry[5] * geo_coef], axis=2)
    return result.reshape(row_count, coef_count, col_count)

def apply_system(field, normal):
    row_count, coef_count, col_count = field.shape
    padded = jnp.pad(field, ((1, 1), (0, 0), (1, 1)))
    beside = padded[2:, :, 1:-1] + padded[:-2, :, 1:-1] + padded[1:-1, :, 2:] + padded[1:-1, :, :-2]
    row_pos = jnp.arange(row_count, dtype=jnp.int32)[:, None]
    col_pos = jnp.arange(col_count, dtype=jnp.int32)[None, :]
    degree = 4.0 - (row_pos == 0).astype(jnp.float32) - (row_pos == row_count - 1).astype(jnp.float32) - (col_pos == 0).astype(jnp.float32) - (col_pos == col_count - 1).astype(jnp.float32)
    return couple(field, normal) + prior_pull * field + smooth_pull * (degree[:, None, :] * field - beside)

def reference(reflect, clear_conf, sun_view, sensor_id, band_gain, sensor_weight, prior):
    date_gain = band_gain[sensor_id]
    date_weight = sensor_weight[sensor_id]
    block_count = DATES // 8

    def add_block(running, block_index):
        first_date = (block_index * 8).astype(jnp.int32)
        term = normal_terms(lax.dynamic_slice_in_dim(reflect, first_date, 8, 0), lax.dynamic_slice_in_dim(clear_conf, first_date, 8, 0), lax.dynamic_slice_in_dim(sun_view, first_date, 8, 0), lax.dynamic_slice_in_dim(date_gain, first_date, 8, 0), lax.dynamic_slice_in_dim(date_weight, first_date, 8, 0))
        return (running + term, None)
    start_sums = jnp.zeros((reflect.shape[2], 24, reflect.shape[3]), jnp.float32)
    sums, _ = lax.scan(add_block, start_sums, jnp.arange(block_count, dtype=jnp.int32))
    sums = sums * (1.0 / DATES)
    normal = sums[:, :6]
    target = sums[:, 6:] + prior_pull * prior
    solution = prior
    residual = target - apply_system(prior, normal)
    direction = residual
    rho_now = jnp.sum(residual * residual)
    for iteration in range(ITERS):
        image = apply_system(direction, normal)
        alpha = rho_now / jnp.sum(direction * image)
        solution = solution + alpha * direction
        residual = residual - alpha * image
        rho_next = jnp.sum(residual * residual)
        direction = residual + rho_next / rho_now * direction
        rho_now = rho_next
    return solution
```

```python
import math

import jax
import jax.numpy as jnp
from jax import lax
from jax.experimental import pallas as pl
from jax.experimental.pallas import tpu as pltpu
from jax.sharding import PartitionSpec as P

DATES = 128

to_radian = math.pi / 18000.0
prior_pull = 0.1
smooth_pull = 0.5
basis_shift = 3.0

LANES = 128
HALVES = 2
ACOS = (
    1.5707963050,
    -0.2145988016,
    0.0889789874,
    -0.0501743046,
    0.0308918810,
    -0.0170881256,
    0.0066700901,
    -0.0012624911,
)


def root(x):
    return x * lax.rsqrt(jnp.maximum(x, 1e-30))


def arccos_over_root(x):
    total = ACOS[-1]
    for coef in ACOS[-2::-1]:
        total = total * x + coef
    return total


def ross_li(sun, view, azim):
    u = (sun - 4500.0) * to_radian
    u2 = u * u
    sin_u = u * (1.0 + u2 * (-1.0 / 6 + u2 * (1.0 / 120 + u2 * (-1.0 / 5040))))
    cos_u = 1.0 + u2 * (-0.5 + u2 * (1.0 / 24 + u2 * (-1.0 / 720 + u2 * (1.0 / 40320))))
    half = math.sqrt(0.5)
    cos_u = cos_u * half
    sin_u = sin_u * half
    sin_sun = cos_u + sin_u
    cos_sun = cos_u - sin_u
    v = view * to_radian
    v2 = v * v
    sin_view = v * (1.0 + v2 * (-1.0 / 6 + v2 * (1.0 / 120)))
    cos_view = 1.0 + v2 * (-0.5 + v2 * (1.0 / 24 + v2 * (-1.0 / 720)))
    a = (9000.0 - azim) * to_radian
    a2 = a * a
    cos_azim = a * (
        1.0
        + a2
        * (
            -1.0 / 6
            + a2
            * (1.0 / 120 + a2 * (-1.0 / 5040 + a2 * (1.0 / 362880 + a2 * (-1.0 / 39916800))))
        )
    )
    cos_pair = cos_sun * cos_view
    sin_pair = sin_sun * sin_view
    cos_total = cos_sun + cos_view
    inverse = 1.0 / (cos_pair * cos_total)
    inv_pair = inverse * cos_total
    inv_total = inverse * cos_pair
    cos_phase = cos_pair + sin_pair * cos_azim
    phase_root = root(1.0 - cos_phase)
    phase_angle = phase_root * arccos_over_root(cos_phase)
    sin_phase = phase_root * root(1.0 + cos_phase)
    volume = ((0.5 * math.pi - phase_angle) * cos_phase + sin_phase) * inv_total - 0.25 * math.pi
    left = sin_sun * cos_view
    right = sin_view * cos_sun
    spread = (
        left * left
        + right * right
        - 2.0 * left * right * cos_azim
        + sin_pair * sin_pair * (1.0 - cos_azim * cos_azim)
    )
    cos_t = jnp.minimum(2.0 * root(spread) * inv_total, 1.0)
    t_root = root(1.0 - cos_t)
    t_part = t_root * (arccos_over_root(cos_t) - root(1.0 + cos_t) * cos_t)
    geometric = inv_pair * (cos_total * (t_part * (1.0 / math.pi) - 1.0) + 0.5 + 0.5 * cos_phase)
    return volume, geometric


def make_kernel(n, dates, bands, total_rows, cols, rows_here):
    quad = 4
    blocks = n // quad
    tall = quad * rows_here
    width = cols // HALVES
    entries = 6 + 3 * bands
    lines = entries * rows_here
    order = []
    low, high = 0, blocks - 1
    while low <= high:
        order.append(high)
        if low != high:
            order.append(low)
        low, high = low + 1, high - 1
    steps = [(block, half) for block in order for half in range(HALVES)]

    def kernel(
        ids_ref,
        gain_ref,
        sensor_ref,
        prior_ref,
        reflect_hbm,
        conf_hbm,
        angle_hbm,
        out_ref,
        reflect_buf,
        conf_buf,
        angle_buf,
        part,
        core_in,
        pair_in,
        block_in,
        sums,
        field,
        halo,
        moment_out,
        moment_in,
        in_sem,
        core_send,
        core_recv,
        pair_send,
        pair_recv,
        block_send,
        block_recv,
        halo_send,
        halo_recv,
        moment_send,
        moment_recv,
    ):
        me = lax.axis_index("rows")
        core = lax.rem(me, 2)
        pair = lax.rem(me // 2, 2)
        zone = me // quad
        has_low = me > 0
        has_high = me < n - 1

        def loads(block):
            window = pl.ds(block * tall, tall)
            return (
                pltpu.make_async_copy(
                    reflect_hbm.at[:, :, window, :], reflect_buf.at[block], in_sem.at[block, 0]
                ),
                pltpu.make_async_copy(
                    conf_hbm.at[:, window, :], conf_buf.at[block], in_sem.at[block, 1]
                ),
                pltpu.make_async_copy(
                    angle_hbm.at[:, :, window, :], angle_buf.at[block], in_sem.at[block, 2]
                ),
            )

        for block in order:
            for copy in loads(block):
                copy.start()

        def remote(src, dst, send, recv, target):
            return pltpu.make_async_remote_copy(
                src_ref=src,
                dst_ref=dst,
                send_sem=send,
                recv_sem=recv,
                device_id={"rows": target},
                device_id_type=pl.DeviceIdType.MESH,
            )

        zero_halo = jnp.zeros(halo.shape[2:], jnp.float32)

        @pl.when(me == 0)
        def _():
            for level in range(4):
                halo[level, 0] = zero_halo

        @pl.when(me == n - 1)
        def _():
            for level in range(4):
                halo[level, 1] = zero_halo

        barrier = pltpu.get_barrier_semaphore()
        for step in range(1, n):
            pl.semaphore_signal(
                barrier,
                inc=1,
                device_id={"rows": lax.rem(me + step, n)},
                device_id_type=pl.DeviceIdType.MESH,
            )

        for row in range(rows_here):
            for kern in range(3):
                for level in range(4):
                    field[level, row, kern] = jnp.zeros((8, cols), jnp.float32)
                for band in range(bands):
                    line = 3 * band + kern
                    field[0, row, kern, band : band + 1, :] = prior_ref[row, line : line + 1, :]

        scale = 0.01 / DATES

        def compute(step):
            block, half = steps[step]
            if half == 0:
                for copy in loads(block):
                    copy.wait()

            def tile(index, carry):
                start = pl.multiple_of(half * width + index * LANES, LANES)
                place = pl.multiple_of(index * LANES, LANES)
                window = pl.ds(start, LANES)
                total = [None] * entries
                for date in range(dates):
                    sensor = ids_ref[me * dates + date]
                    date_scale = sensor_ref[sensor] * scale
                    sun = angle_buf[block, date, 0, :, window].astype(jnp.float32)
                    view = angle_buf[block, date, 1, :, window].astype(jnp.float32)
                    azim = angle_buf[block, date, 2, :, window].astype(jnp.float32)
                    volume, geometric = ross_li(sun, view, azim)
                    weight = conf_buf[block, date, :, window].astype(jnp.float32) * date_scale
                    weighted_vol = weight * volume
                    weighted_geo = weight * geometric
                    terms = [
                        weight,
                        weighted_vol,
                        weighted_geo,
                        weighted_vol * volume,
                        weighted_vol * geometric,
                        weighted_geo * geometric,
                    ] + [None] * (3 * bands)
                    for band in range(bands):
                        signal = (
                            reflect_buf[block, date, band, :, window].astype(jnp.float32)
                            * gain_ref[sensor, band]
                        )
                        terms[6 + band] = weight * signal
                        terms[6 + bands + band] = weighted_vol * signal
                        terms[6 + 2 * bands + band] = weighted_geo * signal
                    total = [t if s is None else s + t for s, t in zip(total, terms)]
                for entry in range(entries):
                    for owner in range(quad):
                        part[
                            block,
                            half,
                            owner % 2,
                            owner // 2,
                            rows_here * entry : rows_here * entry + rows_here,
                            pl.ds(place, LANES),
                        ] = total[entry][owner * rows_here : (owner + 1) * rows_here]
                return carry

            lax.fori_loop(0, width // LANES, tile, 0)

        def core_copy(step):
            block, half = steps[step]
            return remote(
                part.at[block, half, 1 - core],
                core_in.at[block, half],
                core_send.at[step],
                core_recv.at[step],
                me + 1 - 2 * core,
            )

        def pair_copy(step):
            block, half = steps[step]
            return remote(
                part.at[block, half, core, 1 - pair],
                pair_in.at[block, half],
                pair_send.at[step],
                pair_recv.at[step],
                me + 2 - 4 * pair,
            )

        def block_copy(step, source):
            block, half = steps[step]
            return remote(
                part.at[block, half, core, pair],
                block_in.at[source, half],
                block_send.at[step],
                block_recv.at[source, half],
                block * quad + lax.rem(me, quad),
            )

        def halo_copy(level, up):
            row = 0 if up else rows_here - 1
            side = 1 if up else 0
            return remote(
                field.at[level, row],
                halo.at[level, side],
                halo_send.at[level, side],
                halo_recv.at[level, side],
                me - 1 if up else me + 1,
            )

        def send_halo(level):
            @pl.when(has_low)
            def _():
                halo_copy(level, True).start()

            @pl.when(has_high)
            def _():
                halo_copy(level, False).start()

        def await_halo(level):
            @pl.when(has_low)
            def _():
                halo_copy(level, False).wait_recv()

            @pl.when(has_high)
            def _():
                halo_copy(level, True).wait_recv()

        count = len(steps)
        for step in range(count + 2):
            if step < count:
                compute(step)
                if step == 0:
                    pl.semaphore_wait(barrier, n - 1)
                    send_halo(0)
                core_copy(step).start()
            if 1 <= step <= count:
                last = step - 1
                block, half = steps[last]
                core_copy(last).wait_recv()
                for side in range(2):
                    part[block, half, core, side] = (
                        part[block, half, core, side] + core_in[block, half, side]
                    )
                pair_copy(last).start()
            if step >= 2:
                last = step - 2
                block, half = steps[last]
                pair_copy(last).wait_recv()
                part[block, half, core, pair] = (
                    part[block, half, core, pair] + pair_in[block, half]
                )

                @pl.when(zone != block)
                def _(last=last):
                    block_copy(last, zone).start()

        for half in range(HALVES):
            step = half
            total = part[zone, half, core, pair]
            for shift in range(1, blocks):
                source = lax.rem(zone + shift, blocks)
                block_copy(step, source).wait_recv()
                total = total + block_in[source, half]
            sums[:, half * width : (half + 1) * width] = total

        lane = lax.broadcasted_iota(jnp.int32, (8, cols), 1)
        first_col = lane == 0
        last_col = lane == cols - 1
        edge_cols = first_col.astype(jnp.float32) + last_col.astype(jnp.float32)

        def normal_entry(row, entry):
            line = rows_here * entry + row
            return jnp.broadcast_to(sums[line : line + 1, :], (8, cols))

        pick = ((0, 1, 2), (1, 3, 4), (2, 4, 5))

        def apply(level):
            await_halo(level)
            result = []
            for row in range(rows_here):
                position = me * rows_here + row
                inside = (
                    4.0
                    - (position == 0).astype(jnp.float32)
                    - (position == total_rows - 1).astype(jnp.float32)
                )
                own = prior_pull + smooth_pull * (inside - edge_cols)
                line = []
                for kern in range(3):
                    here = field[level, row, kern]
                    above = halo[level, 0, kern] if row == 0 else field[level, row - 1, kern]
                    below = (
                        halo[level, 1, kern]
                        if row == rows_here - 1
                        else field[level, row + 1, kern]
                    )
                    before = jnp.where(first_col, 0.0, pltpu.roll(here, 1, 1))
                    after = jnp.where(last_col, 0.0, pltpu.roll(here, cols - 1, 1))
                    image = own * here - smooth_pull * (above + below + before + after)
                    for other in range(3):
                        image = image + normal_entry(row, pick[kern][other]) * field[level, row, other]
                    line.append(image)
                result.append(line)
            return result

        cells = [(row, kern) for row in range(rows_here) for kern in range(3)]
        image = apply(0)
        for row, kern in cells:
            for band in range(bands):
                line = rows_here * (6 + bands * kern + band) + row
                field[1, row, kern, band : band + 1, :] = sums[line : line + 1, :]
        for row, kern in cells:
            field[1, row, kern] = (
                field[1, row, kern] + prior_pull * field[0, row, kern] - image[row][kern]
            )
        send_halo(1)

        def inner(left, right):
            total = None
            for row, kern in cells:
                term = left(row, kern) * right(row, kern)
                total = term if total is None else total + term
            return jnp.sum(jnp.sum(total, axis=0, keepdims=True), axis=1, keepdims=True)

        def stored(level):
            return lambda row, kern: field[level, row, kern]

        moments = [inner(stored(1), stored(1))]
        for level in (1, 2):
            image = apply(level)
            for row, kern in cells:
                field[level + 1, row, kern] = image[row][kern] - basis_shift * field[level, row, kern]
            send_halo(level + 1)
            moments.append(inner(stored(level), stored(level + 1)))
            moments.append(inner(stored(level + 1), stored(level + 1)))
        image = apply(3)
        moments.append(
            inner(
                stored(3),
                lambda row, kern: image[row][kern] - basis_shift * field[3, row, kern],
            )
        )
        small_lane = lax.broadcasted_iota(jnp.int32, (1, LANES), 1)
        packed = jnp.zeros((1, LANES), jnp.float32)
        for index, value in enumerate(moments):
            packed = jnp.where(small_lane == index, value, packed)
        moment_out[...] = packed

        def moment_copy(target, source):
            return remote(
                moment_out,
                moment_in.at[source],
                moment_send.at[target],
                moment_recv.at[source],
                target,
            )

        for step in range(1, n):
            moment_copy(lax.rem(me + step, n), me).start()
        gathered = packed
        for step in range(1, n):
            source = lax.rem(me + step, n)
            moment_copy(source, source).wait_recv()
            gathered = gathered + moment_in[source]
        m = [
            jnp.sum(jnp.where(small_lane == index, gathered, 0.0), axis=1, keepdims=True)
            for index in range(len(moments))
        ]

        def form(coefs, with_operator):
            total = 0.0
            for i, a in enumerate(coefs):
                for j, b in enumerate(coefs):
                    moment = m[i + j]
                    if with_operator:
                        moment = m[i + j + 1] + basis_shift * moment
                    total = total + a * b * moment
            return total

        one = jnp.ones((1, 1), jnp.float32)
        residual = [one]
        direction = [one]
        answer = [0.0, 0.0, 0.0]
        rho = m[0]
        for iteration in range(3):
            alpha = rho / form(direction, True)
            answer = [
                a + (alpha * direction[i] if i < len(direction) else 0.0)
                for i, a in enumerate(answer)
            ]
            if iteration < 2:
                image = [basis_shift * d for d in direction] + [0.0]
                for i, d in enumerate(direction):
                    image[i + 1] = image[i + 1] + d
                residual = [
                    (residual[i] if i < len(residual) else 0.0) - alpha * image[i]
                    for i in range(len(image))
                ]
                rho_next = form(residual, False)
                ratio = rho_next / rho
                direction = [
                    residual[i] + (ratio * direction[i] if i < len(direction) else 0.0)
                    for i in range(len(residual))
                ]
                rho = rho_next
        for row, kern in cells:
            value = field[0, row, kern]
            for level in range(3):
                value = value + answer[level] * field[level + 1, row, kern]
            for band in range(bands):
                line = 3 * band + kern
                out_ref[row, line : line + 1, :] = value[band : band + 1]

        for step in range(count):
            core_copy(step).wait_send()
            pair_copy(step).wait_send()

            @pl.when(zone != steps[step][0])
            def _(step=step):
                block_copy(step, zone).wait_send()

        for level in range(4):

            @pl.when(has_low)
            def _(level=level):
                halo_copy(level, True).wait_send()

            @pl.when(has_high)
            def _(level=level):
                halo_copy(level, False).wait_send()

        for step in range(1, n):
            moment_copy(lax.rem(me + step, n), me).wait_send()

    count = len(steps)
    f32 = jnp.float32
    dma = pltpu.SemaphoreType.DMA
    scratch = [
        pltpu.VMEM((blocks, dates, bands, tall, cols), jnp.bfloat16),
        pltpu.VMEM((blocks, dates, tall, cols), jnp.int32),
        pltpu.VMEM((blocks, dates, 3, tall, cols), jnp.int32),
        pltpu.VMEM((blocks, HALVES, 2, 2, lines, width), f32),
        pltpu.VMEM((blocks, HALVES, 2, lines, width), f32),
        pltpu.VMEM((blocks, HALVES, lines, width), f32),
        pltpu.VMEM((blocks, HALVES, lines, width), f32),
        pltpu.VMEM((lines, cols), f32),
        pltpu.VMEM((4, rows_here, 3, 8, cols), f32),
        pltpu.VMEM((4, 2, 3, 8, cols), f32),
        pltpu.VMEM((1, LANES), f32),
        pltpu.VMEM((n, 1, LANES), f32),
        dma((blocks, 3)),
        dma((count,)),
        dma((count,)),
        dma((count,)),
        dma((count,)),
        dma((count,)),
        dma((blocks, HALVES)),
        dma((4, 2)),
        dma((4, 2)),
        dma((n,)),
        dma((n,)),
    ]
    return kernel, scratch


def solution(mesh):
    n = mesh.shape["rows"]

    def on_device(reflect, clear_conf, sun_view, sensor_id, band_gain, sensor_weight, prior):
        dates, bands, total_rows, cols = reflect.shape
        kernel, scratch = make_kernel(n, dates, bands, total_rows, cols, prior.shape[0])
        smem = pl.BlockSpec(memory_space=pltpu.SMEM)
        vmem = pl.BlockSpec(memory_space=pltpu.VMEM)
        hbm = pl.BlockSpec(memory_space=pl.ANY)
        return pl.pallas_call(
            kernel,
            out_shape=jax.ShapeDtypeStruct(prior.shape, jnp.float32),
            in_specs=[smem, smem, smem, vmem, hbm, hbm, hbm],
            out_specs=vmem,
            scratch_shapes=scratch,
            compiler_params=pltpu.CompilerParams(
                collective_id=0, has_side_effects=True, vmem_limit_bytes=60 * 1024 * 1024
            ),
        )(sensor_id, band_gain, sensor_weight, prior, reflect, clear_conf, sun_view)

    return jax.shard_map(
        on_device,
        mesh=mesh,
        in_specs=(
            P("rows", None, None, "tiles"),
            P("rows", None, "tiles"),
            P("rows", None, None, "tiles"),
            P(),
            P(),
            P(),
            P("rows", None, "tiles"),
        ),
        out_specs=P("rows", None, "tiles"),
        check_vma=False,
    )
```

```python
import math

import jax
import jax.numpy as jnp
from jax import lax
from jax.experimental import pallas as pl
from jax.experimental.pallas import tpu as pltpu
from jax.sharding import PartitionSpec as P

DATES = 128

to_radian = math.pi / 18000.0
prior_pull = 0.1
smooth_pull = 0.5
basis_shift = 3.0

geo_centre = -1.2

LANES = 128
HALVES = 2
ACOS = (
    1.5707963050,
    -0.2145988016,
    0.0889789874,
    -0.0501743046,
    0.0308918810,
    -0.0170881256,
    0.0066700901,
    -0.0012624911,
)


def root(x):
    return x * lax.rsqrt(jnp.maximum(x, 1e-30))


def arccos_over_root(x):
    total = ACOS[-1]
    for coef in ACOS[-2::-1]:
        total = total * x + coef
    return total


def ross_li(sun, view, azim):
    u = (sun - 4500.0) * to_radian
    u2 = u * u
    sin_u = u * (1.0 + u2 * (-1.0 / 6 + u2 * (1.0 / 120 + u2 * (-1.0 / 5040))))
    cos_u = 1.0 + u2 * (-0.5 + u2 * (1.0 / 24 + u2 * (-1.0 / 720 + u2 * (1.0 / 40320))))
    half = math.sqrt(0.5)
    cos_u = cos_u * half
    sin_u = sin_u * half
    sin_sun = cos_u + sin_u
    cos_sun = cos_u - sin_u
    v = view * to_radian
    v2 = v * v
    sin_view = v * (1.0 + v2 * (-1.0 / 6 + v2 * (1.0 / 120)))
    cos_view = 1.0 + v2 * (-0.5 + v2 * (1.0 / 24 + v2 * (-1.0 / 720)))
    a = (9000.0 - azim) * to_radian
    a2 = a * a
    cos_azim = a * (
        1.0
        + a2
        * (
            -1.0 / 6
            + a2
            * (1.0 / 120 + a2 * (-1.0 / 5040 + a2 * (1.0 / 362880 + a2 * (-1.0 / 39916800))))
        )
    )
    cos_pair = cos_sun * cos_view
    sin_pair = sin_sun * sin_view
    cos_total = cos_sun + cos_view
    inverse = 1.0 / (cos_pair * cos_total)
    inv_pair = inverse * cos_total
    inv_total = inverse * cos_pair
    cos_phase = cos_pair + sin_pair * cos_azim
    phase_root = root(1.0 - cos_phase)
    phase_angle = phase_root * arccos_over_root(cos_phase)
    sin_phase = phase_root * root(1.0 + cos_phase)
    volume = ((0.5 * math.pi - phase_angle) * cos_phase + sin_phase) * inv_total - 0.25 * math.pi
    left = sin_sun * cos_view
    right = sin_view * cos_sun
    spread = (
        left * left
        + right * right
        - 2.0 * left * right * cos_azim
        + sin_pair * sin_pair * (1.0 - cos_azim * cos_azim)
    )
    cos_t = jnp.minimum(2.0 * root(spread) * inv_total, 1.0)
    t_root = root(1.0 - cos_t)
    t_part = t_root * (arccos_over_root(cos_t) - root(1.0 + cos_t) * cos_t)
    geometric = inv_pair * (cos_total * (t_part * (1.0 / math.pi) - 1.0) + 0.5 + 0.5 * cos_phase)
    return volume, geometric - geo_centre


def make_kernel(n, dates, bands, total_rows, cols, rows_here):
    quad = 4
    blocks = n // quad
    tall = quad * rows_here
    width = cols // HALVES
    entries = 6 + 3 * bands
    lines = entries * rows_here
    third = lines // 3
    normal_at = (0, 2 * (2 + bands), 1, 2 * (2 + bands) + 1, 3 + bands, 2 + bands)
    signal_at = (2, 2 * (2 + bands) + 2, 4 + bands)
    order = []
    low, high = 0, blocks - 1
    while low <= high:
        order.append(high)
        if low != high:
            order.append(low)
        low, high = low + 1, high - 1
    steps = [(block, half) for half in range(HALVES) for block in order]

    def kernel(
        ids_ref,
        gain_ref,
        sensor_ref,
        prior_ref,
        reflect_hbm,
        conf_hbm,
        angle_hbm,
        out_ref,
        reflect_buf,
        conf_buf,
        angle_buf,
        part,
        core_in,
        pair_in,
        block_in,
        sums,
        field,
        halo,
        moment_out,
        moment_in,
        pair_half_out,
        pair_half_in,
        block_half_out,
        block_half_in,
        pair_half_send,
        pair_half_recv,
        block_half_send,
        block_half_recv,
        in_sem,
        core_send,
        core_recv,
        pair_send,
        pair_recv,
        block_send,
        block_recv,
        halo_send,
        halo_recv,
        moment_send,
        moment_recv,
    ):
        me = lax.axis_index("rows")
        core = lax.rem(me, 2)
        pair = lax.rem(me // 2, 2)
        zone = me // quad
        has_low = me > 0
        has_high = me < n - 1

        def loads(block):
            window = pl.ds(block * tall, tall)
            return (
                pltpu.make_async_copy(
                    reflect_hbm.at[:, :, window, :], reflect_buf.at[block], in_sem.at[block, 0]
                ),
                pltpu.make_async_copy(
                    conf_hbm.at[:, window, :], conf_buf.at[block], in_sem.at[block, 1]
                ),
                pltpu.make_async_copy(
                    angle_hbm.at[:, :, window, :], angle_buf.at[block], in_sem.at[block, 2]
                ),
            )

        for block in order:
            for copy in loads(block):
                copy.start()

        def remote(src, dst, send, recv, target):
            return pltpu.make_async_remote_copy(
                src_ref=src,
                dst_ref=dst,
                send_sem=send,
                recv_sem=recv,
                device_id={"rows": target},
                device_id_type=pl.DeviceIdType.MESH,
            )

        zero_halo = jnp.zeros(halo.shape[2:], jnp.float32)

        @pl.when(me == 0)
        def _():
            for level in range(4):
                halo[level, 0] = zero_halo

        @pl.when(me == n - 1)
        def _():
            for level in range(4):
                halo[level, 1] = zero_halo

        barrier = pltpu.get_barrier_semaphore()
        for step in range(1, n):
            pl.semaphore_signal(
                barrier,
                inc=1,
                device_id={"rows": lax.rem(me + step, n)},
                device_id_type=pl.DeviceIdType.MESH,
            )

        for row in range(rows_here):
            for kern in range(3):
                for level in range(4):
                    field[level, row, kern] = jnp.zeros((8, cols), jnp.float32)
                for band in range(bands):
                    line = 3 * band + kern
                    field[0, row, kern, band : band + 1, :] = prior_ref[line, row : row + 1, :]

        scale = 0.01 / DATES

        def compute(step):
            block, half = steps[step]
            if half == 0:
                for copy in loads(block):
                    copy.wait()

            def tile(index, carry):
                start = pl.multiple_of(half * width + index * LANES, LANES)
                place = pl.multiple_of(index * LANES, LANES)
                window = pl.ds(start, LANES)
                total = [None] * entries
                for date in range(dates):
                    sensor = ids_ref[me * dates + date]
                    date_scale = sensor_ref[sensor] * scale
                    sun = angle_buf[block, date, 0, :, window].astype(jnp.float32)
                    view = angle_buf[block, date, 1, :, window].astype(jnp.float32)
                    azim = angle_buf[block, date, 2, :, window].astype(jnp.float32)
                    volume, geometric = ross_li(sun, view, azim)
                    weight = conf_buf[block, date, :, window].astype(jnp.float32) * date_scale
                    weighted_vol = weight * volume
                    weighted_geo = weight * geometric
                    terms = [None] * entries
                    products = (
                        weight,
                        weighted_vol,
                        weighted_geo,
                        weighted_vol * volume,
                        weighted_vol * geometric,
                        weighted_geo * geometric,
                    )
                    for spot, product in zip(normal_at, products):
                        terms[spot] = product
                    for band in range(bands):
                        signal = (
                            reflect_buf[block, date, band, :, window].astype(jnp.float32)
                            * gain_ref[sensor, band]
                        )
                        terms[signal_at[0] + band] = weight * signal
                        terms[signal_at[1] + band] = weighted_vol * signal
                        terms[signal_at[2] + band] = weighted_geo * signal
                    total = [t if s is None else s + t for s, t in zip(total, terms)]
                for entry in range(entries):
                    for owner in range(quad):
                        part[
                            block,
                            half,
                            owner % 2,
                            owner // 2,
                            rows_here * entry : rows_here * entry + rows_here,
                            pl.ds(place, LANES),
                        ] = total[entry][owner * rows_here : (owner + 1) * rows_here]
                return carry

            lax.fori_loop(0, width // LANES, tile, 0)

        def core_copy(step):
            block, half = steps[step]
            return remote(
                part.at[block, half, 1 - core],
                core_in.at[block, half],
                core_send.at[step],
                core_recv.at[step],
                me + 1 - 2 * core,
            )

        def pair_copies(step):
            block, half = steps[step]
            target = me + 2 - 4 * pair
            return (
                remote(
                    part.at[block, half, core, 1 - pair, 0:third],
                    pair_in.at[block, half],
                    pair_send.at[step],
                    pair_recv.at[step],
                    target,
                ),
                remote(
                    pair_half_out.at[block, half],
                    pair_half_in.at[block, half],
                    pair_half_send.at[step],
                    pair_half_recv.at[step],
                    target,
                ),
            )

        def block_copies(step, source):
            block, half = steps[step]
            target = block * quad + lax.rem(me, quad)
            return (
                remote(
                    part.at[block, half, core, pair, 0 : 2 * third],
                    block_in.at[source, half],
                    block_send.at[step],
                    block_recv.at[source, half],
                    target,
                ),
                remote(
                    block_half_out.at[block, half],
                    block_half_in.at[source, half],
                    block_half_send.at[step],
                    block_half_recv.at[source, half],
                    target,
                ),
            )

        def halo_copy(level, up):
            row = 0 if up else rows_here - 1
            side = 1 if up else 0
            return remote(
                field.at[level, row],
                halo.at[level, side],
                halo_send.at[level, side],
                halo_recv.at[level, side],
                me - 1 if up else me + 1,
            )

        def send_halo(level):
            @pl.when(has_low)
            def _():
                halo_copy(level, True).start()

            @pl.when(has_high)
            def _():
                halo_copy(level, False).start()

        def await_halo(level):
            @pl.when(has_low)
            def _():
                halo_copy(level, False).wait_recv()

            @pl.when(has_high)
            def _():
                halo_copy(level, True).wait_recv()

        count = len(steps)
        for step in range(count + 2):
            if step < count:
                compute(step)
                if step == 0:
                    pl.semaphore_wait(barrier, n - 1)
                    send_halo(0)
                core_copy(step).start()
            if 1 <= step <= count:
                last = step - 1
                block, half = steps[last]
                core_copy(last).wait_recv()
                other = 1 - pair
                part[block, half, core, other, 0:third] = (
                    part[block, half, core, other, 0:third] + core_in[block, half, other, 0:third]
                )
                pair_half_out[block, half] = (
                    part[block, half, core, other, third:lines]
                    + core_in[block, half, other, third:lines]
                ).astype(jnp.bfloat16)
                for copy in pair_copies(last):
                    copy.start()
                part[block, half, core, pair] = (
                    part[block, half, core, pair] + core_in[block, half, pair]
                )
            if step >= 2:
                last = step - 2
                block, half = steps[last]
                for copy in pair_copies(last):
                    copy.wait_recv()
                part[block, half, core, pair, 0:third] = (
                    part[block, half, core, pair, 0:third] + pair_in[block, half]
                )
                rest = part[block, half, core, pair, third:lines] + pair_half_in[
                    block, half
                ].astype(jnp.float32)
                part[block, half, core, pair, third:lines] = rest
                block_half_out[block, half] = rest[third:].astype(jnp.bfloat16)

                @pl.when(zone != block)
                def _(last=last):
                    for copy in block_copies(last, zone):
                        copy.start()

        for half in range(HALVES):
            step = steps.index((0, half))
            total = part[zone, half, core, pair, 0 : 2 * third]
            small = part[zone, half, core, pair, 2 * third : lines]
            for shift in range(1, blocks):
                source = lax.rem(zone + shift, blocks)
                for copy in block_copies(step, source):
                    copy.wait_recv()
                total = total + block_in[source, half]
                small = small + block_half_in[source, half].astype(jnp.float32)
            sums[0 : 2 * third, half * width : (half + 1) * width] = total
            sums[2 * third : lines, half * width : (half + 1) * width] = small

        def lines_of(spot, length=1):
            return pl.ds(rows_here * spot, rows_here * length)

        n00, n01, n02, _, n12, n22 = (lines_of(spot) for spot in normal_at)
        sums[n22] = sums[n22] + 2.0 * geo_centre * sums[n02] + geo_centre**2 * sums[n00]
        sums[n12] = sums[n12] + geo_centre * sums[n01]
        sums[n02] = sums[n02] + geo_centre * sums[n00]
        geo_lines = lines_of(signal_at[2], bands)
        sums[geo_lines] = sums[geo_lines] + geo_centre * sums[lines_of(signal_at[0], bands)]

        lane = lax.broadcasted_iota(jnp.int32, (8, cols), 1)
        first_col = lane == 0
        last_col = lane == cols - 1
        edge_cols = first_col.astype(jnp.float32) + last_col.astype(jnp.float32)

        def normal_entry(row, entry):
            line = rows_here * normal_at[entry] + row
            return jnp.broadcast_to(sums[line : line + 1, :], (8, cols))

        pick = ((0, 1, 2), (1, 3, 4), (2, 4, 5))

        def apply(level):
            result = []
            for row in range(rows_here):
                position = me * rows_here + row
                inside = (
                    4.0
                    - (position == 0).astype(jnp.float32)
                    - (position == total_rows - 1).astype(jnp.float32)
                )
                own = prior_pull + smooth_pull * (inside - edge_cols)
                line = []
                for kern in range(3):
                    here = field[level, row, kern]
                    before = jnp.where(first_col, 0.0, pltpu.roll(here, 1, 1))
                    after = jnp.where(last_col, 0.0, pltpu.roll(here, cols - 1, 1))
                    beside = before + after
                    if row > 0:
                        beside = beside + field[level, row - 1, kern]
                    if row < rows_here - 1:
                        beside = beside + field[level, row + 1, kern]
                    image = own * here - smooth_pull * beside
                    for other in range(3):
                        image = image + normal_entry(row, pick[kern][other]) * field[level, row, other]
                    line.append(image)
                result.append(line)
            await_halo(level)
            for kern in range(3):
                result[0][kern] = result[0][kern] - smooth_pull * halo[level, 0, kern]
                result[-1][kern] = result[-1][kern] - smooth_pull * halo[level, 1, kern]
            return result

        cells = [(row, kern) for row in range(rows_here) for kern in range(3)]
        image = apply(0)
        for row, kern in cells:
            for band in range(bands):
                line = rows_here * (signal_at[kern] + band) + row
                field[1, row, kern, band : band + 1, :] = sums[line : line + 1, :]
        for row, kern in cells:
            field[1, row, kern] = (
                field[1, row, kern] + prior_pull * field[0, row, kern] - image[row][kern]
            )
        send_halo(1)

        def inner(left, right):
            total = None
            for row, kern in cells:
                term = left(row, kern) * right(row, kern)
                total = term if total is None else total + term
            return jnp.sum(jnp.sum(total, axis=0, keepdims=True), axis=1, keepdims=True)

        def stored(level):
            return lambda row, kern: field[level, row, kern]

        moments = [inner(stored(1), stored(1))]
        for level in (1, 2):
            image = apply(level)
            for row, kern in cells:
                field[level + 1, row, kern] = image[row][kern] - basis_shift * field[level, row, kern]
            send_halo(level + 1)
            moments.append(inner(stored(level), stored(level + 1)))
            moments.append(inner(stored(level + 1), stored(level + 1)))
        image = apply(3)
        moments.append(
            inner(
                stored(3),
                lambda row, kern: image[row][kern] - basis_shift * field[3, row, kern],
            )
        )
        small_lane = lax.broadcasted_iota(jnp.int32, (1, LANES), 1)
        packed = jnp.zeros((1, LANES), jnp.float32)
        for index, value in enumerate(moments):
            packed = jnp.where(small_lane == index, value, packed)
        moment_out[...] = packed

        def moment_copy(target, source):
            return remote(
                moment_out,
                moment_in.at[source],
                moment_send.at[target],
                moment_recv.at[source],
                target,
            )

        for step in range(1, n):
            moment_copy(lax.rem(me + step, n), me).start()
        gathered = packed
        for step in range(1, n):
            source = lax.rem(me + step, n)
            moment_copy(source, source).wait_recv()
            gathered = gathered + moment_in[source]
        m = [
            jnp.sum(jnp.where(small_lane == index, gathered, 0.0), axis=1, keepdims=True)
            for index in range(len(moments))
        ]

        def form(coefs, with_operator):
            total = 0.0
            for i, a in enumerate(coefs):
                for j, b in enumerate(coefs):
                    moment = m[i + j]
                    if with_operator:
                        moment = m[i + j + 1] + basis_shift * moment
                    total = total + a * b * moment
            return total

        one = jnp.ones((1, 1), jnp.float32)
        residual = [one]
        direction = [one]
        answer = [0.0, 0.0, 0.0]
        rho = m[0]
        for iteration in range(3):
            alpha = rho / form(direction, True)
            answer = [
                a + (alpha * direction[i] if i < len(direction) else 0.0)
                for i, a in enumerate(answer)
            ]
            if iteration < 2:
                image = [basis_shift * d for d in direction] + [0.0]
                for i, d in enumerate(direction):
                    image[i + 1] = image[i + 1] + d
                residual = [
                    (residual[i] if i < len(residual) else 0.0) - alpha * image[i]
                    for i in range(len(image))
                ]
                rho_next = form(residual, False)
                ratio = rho_next / rho
                direction = [
                    residual[i] + (ratio * direction[i] if i < len(direction) else 0.0)
                    for i in range(len(residual))
                ]
                rho = rho_next
        for row, kern in cells:
            value = field[0, row, kern]
            for level in range(3):
                value = value + answer[level] * field[level + 1, row, kern]
            for band in range(bands):
                line = 3 * band + kern
                out_ref[line, row : row + 1, :] = value[band : band + 1]

        for step in range(count):
            core_copy(step).wait_send()
            for copy in pair_copies(step):
                copy.wait_send()

            @pl.when(zone != steps[step][0])
            def _(step=step):
                for copy in block_copies(step, zone):
                    copy.wait_send()

        for level in range(4):

            @pl.when(has_low)
            def _(level=level):
                halo_copy(level, True).wait_send()

            @pl.when(has_high)
            def _(level=level):
                halo_copy(level, False).wait_send()

        for step in range(1, n):
            moment_copy(lax.rem(me + step, n), me).wait_send()

    count = len(steps)
    f32 = jnp.float32
    dma = pltpu.SemaphoreType.DMA
    scratch = [
        pltpu.VMEM((blocks, dates, bands, tall, cols), jnp.bfloat16),
        pltpu.VMEM((blocks, dates, tall, cols), jnp.int32),
        pltpu.VMEM((blocks, dates, 3, tall, cols), jnp.int32),
        pltpu.VMEM((blocks, HALVES, 2, 2, lines, width), f32),
        pltpu.VMEM((blocks, HALVES, 2, lines, width), f32),
        pltpu.VMEM((blocks, HALVES, lines // 3, width), f32),
        pltpu.VMEM((blocks, HALVES, 2 * lines // 3, width), f32),
        pltpu.VMEM((lines, cols), f32),
        pltpu.VMEM((4, rows_here, 3, 8, cols), f32),
        pltpu.VMEM((4, 2, 3, 8, cols), f32),
        pltpu.VMEM((1, LANES), f32),
        pltpu.VMEM((n, 1, LANES), f32),
        pltpu.VMEM((blocks, HALVES, 2 * lines // 3, width), jnp.bfloat16),
        pltpu.VMEM((blocks, HALVES, 2 * lines // 3, width), jnp.bfloat16),
        pltpu.VMEM((blocks, HALVES, lines // 3, width), jnp.bfloat16),
        pltpu.VMEM((blocks, HALVES, lines // 3, width), jnp.bfloat16),
        dma((count,)),
        dma((count,)),
        dma((count,)),
        dma((blocks, HALVES)),
        dma((blocks, 3)),
        dma((count,)),
        dma((count,)),
        dma((count,)),
        dma((count,)),
        dma((count,)),
        dma((blocks, HALVES)),
        dma((4, 2)),
        dma((4, 2)),
        dma((n,)),
        dma((n,)),
    ]
    return kernel, scratch


def solution(mesh):
    n = mesh.shape["rows"]

    def on_device(reflect, clear_conf, sun_view, sensor_id, band_gain, sensor_weight, prior):
        dates, bands, total_rows, cols = reflect.shape
        kernel, scratch = make_kernel(n, dates, bands, total_rows, cols, prior.shape[0])
        smem = pl.BlockSpec(memory_space=pltpu.SMEM)
        vmem = pl.BlockSpec(memory_space=pltpu.VMEM)
        hbm = pl.BlockSpec(memory_space=pl.ANY)
        stored = prior.transpose(1, 0, 2)
        solved = pl.pallas_call(
            kernel,
            out_shape=jax.ShapeDtypeStruct(stored.shape, jnp.float32),
            in_specs=[smem, smem, smem, vmem, hbm, hbm, hbm],
            out_specs=vmem,
            scratch_shapes=scratch,
            compiler_params=pltpu.CompilerParams(
                collective_id=0, has_side_effects=True, vmem_limit_bytes=60 * 1024 * 1024
            ),
        )(sensor_id, band_gain, sensor_weight, stored, reflect, clear_conf, sun_view)
        return solved.transpose(1, 0, 2)

    return jax.shard_map(
        on_device,
        mesh=mesh,
        in_specs=(
            P("rows", None, None, "tiles"),
            P("rows", None, "tiles"),
            P("rows", None, None, "tiles"),
            P(),
            P(),
            P(),
            P("rows", None, "tiles"),
        ),
        out_specs=P("rows", None, "tiles"),
        check_vma=False,
    )
```

```python
import math

import jax
import jax.numpy as jnp
from jax import lax
from jax.experimental import pallas as pl
from jax.experimental.pallas import tpu as pltpu
from jax.sharding import PartitionSpec as P

DATES = 128

to_radian = math.pi / 18000.0
prior_pull = 0.1
smooth_pull = 0.5
basis_shift = 3.0

geo_centre = -1.2

LANES = 128
HALVES = 2
CORE_LAG = 2
PAIR_LAG = 5
ACOS = (
    1.5707963050,
    -0.2145988016,
    0.0889789874,
    -0.0501743046,
    0.0308918810,
    -0.0170881256,
    0.0066700901,
    -0.0012624911,
)


def root(x):
    return x * lax.rsqrt(jnp.maximum(x, 1e-30))


def arccos_over_root(x):
    total = ACOS[-1]
    for coef in ACOS[-2::-1]:
        total = total * x + coef
    return total


def ross_li(sun, view, azim):
    u = (sun - 4500.0) * to_radian
    u2 = u * u
    sin_u = u * (1.0 + u2 * (-1.0 / 6 + u2 * (1.0 / 120 + u2 * (-1.0 / 5040))))
    cos_u = 1.0 + u2 * (-0.5 + u2 * (1.0 / 24 + u2 * (-1.0 / 720 + u2 * (1.0 / 40320))))
    half = math.sqrt(0.5)
    cos_u = cos_u * half
    sin_u = sin_u * half
    sin_sun = cos_u + sin_u
    cos_sun = cos_u - sin_u
    v = view * to_radian
    v2 = v * v
    sin_view = v * (1.0 + v2 * (-1.0 / 6 + v2 * (1.0 / 120)))
    cos_view = 1.0 + v2 * (-0.5 + v2 * (1.0 / 24 + v2 * (-1.0 / 720)))
    a = (9000.0 - azim) * to_radian
    a2 = a * a
    cos_azim = a * (
        1.0
        + a2
        * (
            -1.0 / 6
            + a2
            * (1.0 / 120 + a2 * (-1.0 / 5040 + a2 * (1.0 / 362880 + a2 * (-1.0 / 39916800))))
        )
    )
    cos_pair = cos_sun * cos_view
    sin_pair = sin_sun * sin_view
    cos_total = cos_sun + cos_view
    inverse = 1.0 / (cos_pair * cos_total)
    inv_pair = inverse * cos_total
    inv_total = inverse * cos_pair
    cos_phase = cos_pair + sin_pair * cos_azim
    phase_root = root(1.0 - cos_phase)
    phase_angle = phase_root * arccos_over_root(cos_phase)
    sin_phase = phase_root * root(1.0 + cos_phase)
    volume = ((0.5 * math.pi - phase_angle) * cos_phase + sin_phase) * inv_total - 0.25 * math.pi
    left = sin_sun * cos_view
    right = sin_view * cos_sun
    spread = (
        left * left
        + right * right
        - 2.0 * left * right * cos_azim
        + sin_pair * sin_pair * (1.0 - cos_azim * cos_azim)
    )
    cos_t = jnp.minimum(2.0 * root(spread) * inv_total, 1.0)
    t_root = root(1.0 - cos_t)
    t_part = t_root * (arccos_over_root(cos_t) - root(1.0 + cos_t) * cos_t)
    geometric = inv_pair * (cos_total * (t_part * (1.0 / math.pi) - 1.0) + 0.5 + 0.5 * cos_phase)
    return volume, geometric - geo_centre


def make_kernel(n, dates, bands, total_rows, cols, rows_here):
    quad = 4
    blocks = n // quad
    tall = quad * rows_here
    width = cols // HALVES
    entries = 6 + 3 * bands
    lines = entries * rows_here
    third = lines // 3
    normal_at = (0, 2 * (2 + bands), 1, 2 * (2 + bands) + 1, 3 + bands, 2 + bands)
    signal_at = (2, 2 * (2 + bands) + 2, 4 + bands)
    order = []
    low, high = 0, blocks - 1
    while low <= high:
        order.append(high)
        if low != high:
            order.append(low)
        low, high = low + 1, high - 1
    steps = [(block, half) for half in range(HALVES) for block in order]

    def kernel(
        ids_ref,
        gain_ref,
        sensor_ref,
        prior_ref,
        reflect_hbm,
        conf_hbm,
        angle_hbm,
        out_ref,
        reflect_buf,
        conf_buf,
        angle_buf,
        part,
        core_in,
        pair_in,
        block_in,
        sums,
        field,
        halo,
        moment_out,
        moment_in,
        pair_half_out,
        pair_half_in,
        block_half_out,
        block_half_in,
        pair_half_send,
        pair_half_recv,
        block_half_send,
        block_half_recv,
        in_sem,
        core_send,
        core_recv,
        pair_send,
        pair_recv,
        block_send,
        block_recv,
        halo_send,
        halo_recv,
        moment_send,
        moment_recv,
    ):
        me = lax.axis_index("rows")
        core = lax.rem(me, 2)
        pair = lax.rem(me // 2, 2)
        zone = me // quad
        has_low = me > 0
        has_high = me < n - 1

        def loads(block):
            window = pl.ds(block * tall, tall)
            return (
                pltpu.make_async_copy(
                    reflect_hbm.at[:, :, window, :], reflect_buf.at[block], in_sem.at[block, 0]
                ),
                pltpu.make_async_copy(
                    conf_hbm.at[:, window, :], conf_buf.at[block], in_sem.at[block, 1]
                ),
                pltpu.make_async_copy(
                    angle_hbm.at[:, :, window, :], angle_buf.at[block], in_sem.at[block, 2]
                ),
            )

        for block in order:
            for copy in loads(block):
                copy.start()

        def remote(src, dst, send, recv, target):
            return pltpu.make_async_remote_copy(
                src_ref=src,
                dst_ref=dst,
                send_sem=send,
                recv_sem=recv,
                device_id={"rows": target},
                device_id_type=pl.DeviceIdType.MESH,
            )

        zero_halo = jnp.zeros(halo.shape[2:], jnp.float32)

        @pl.when(me == 0)
        def _():
            for level in range(4):
                halo[level, 0] = zero_halo

        @pl.when(me == n - 1)
        def _():
            for level in range(4):
                halo[level, 1] = zero_halo

        barrier = pltpu.get_barrier_semaphore()
        for step in range(1, n):
            pl.semaphore_signal(
                barrier,
                inc=1,
                device_id={"rows": lax.rem(me + step, n)},
                device_id_type=pl.DeviceIdType.MESH,
            )

        for row in range(rows_here):
            for kern in range(3):
                for level in range(4):
                    field[level, row, kern] = jnp.zeros((8, cols), jnp.float32)
                for band in range(bands):
                    line = 3 * band + kern
                    field[0, row, kern, band : band + 1, :] = prior_ref[line, row : row + 1, :]

        scale = 0.01 / DATES

        def compute(step):
            block, half = steps[step]
            if half == 0:
                for copy in loads(block):
                    copy.wait()

            def tile(index, carry):
                start = pl.multiple_of(half * width + index * LANES, LANES)
                place = pl.multiple_of(index * LANES, LANES)
                window = pl.ds(start, LANES)
                total = [None] * entries
                for date in range(dates):
                    sensor = ids_ref[me * dates + date]
                    date_scale = sensor_ref[sensor] * scale
                    sun = angle_buf[block, date, 0, :, window].astype(jnp.float32)
                    view = angle_buf[block, date, 1, :, window].astype(jnp.float32)
                    azim = angle_buf[block, date, 2, :, window].astype(jnp.float32)
                    volume, geometric = ross_li(sun, view, azim)
                    weight = conf_buf[block, date, :, window].astype(jnp.float32) * date_scale
                    weighted_vol = weight * volume
                    weighted_geo = weight * geometric
                    terms = [None] * entries
                    products = (
                        weight,
                        weighted_vol,
                        weighted_geo,
                        weighted_vol * volume,
                        weighted_vol * geometric,
                        weighted_geo * geometric,
                    )
                    for spot, product in zip(normal_at, products):
                        terms[spot] = product
                    for band in range(bands):
                        signal = (
                            reflect_buf[block, date, band, :, window].astype(jnp.float32)
                            * gain_ref[sensor, band]
                        )
                        terms[signal_at[0] + band] = weight * signal
                        terms[signal_at[1] + band] = weighted_vol * signal
                        terms[signal_at[2] + band] = weighted_geo * signal
                    total = [t if s is None else s + t for s, t in zip(total, terms)]
                for entry in range(entries):
                    for owner in range(quad):
                        part[
                            block,
                            half,
                            owner % 2,
                            owner // 2,
                            rows_here * entry : rows_here * entry + rows_here,
                            pl.ds(place, LANES),
                        ] = total[entry][owner * rows_here : (owner + 1) * rows_here]
                return carry

            lax.fori_loop(0, width // LANES, tile, 0)

        def core_copy(step):
            block, half = steps[step]
            return remote(
                part.at[block, half, 1 - core],
                core_in.at[block, half],
                core_send.at[step],
                core_recv.at[step],
                me + 1 - 2 * core,
            )

        def pair_copies(step):
            block, half = steps[step]
            target = me + 2 - 4 * pair
            return (
                remote(
                    part.at[block, half, core, 1 - pair, 0:third],
                    pair_in.at[block, half],
                    pair_send.at[step],
                    pair_recv.at[step],
                    target,
                ),
                remote(
                    pair_half_out.at[block, half],
                    pair_half_in.at[block, half],
                    pair_half_send.at[step],
                    pair_half_recv.at[step],
                    target,
                ),
            )

        def block_copies(step, source):
            block, half = steps[step]
            target = block * quad + lax.rem(me, quad)
            return (
                remote(
                    part.at[block, half, core, pair, 0 : 2 * third],
                    block_in.at[source, half],
                    block_send.at[step],
                    block_recv.at[source, half],
                    target,
                ),
                remote(
                    block_half_out.at[block, half],
                    block_half_in.at[source, half],
                    block_half_send.at[step],
                    block_half_recv.at[source, half],
                    target,
                ),
            )

        def halo_copy(level, up):
            row = 0 if up else rows_here - 1
            side = 1 if up else 0
            return remote(
                field.at[level, row],
                halo.at[level, side],
                halo_send.at[level, side],
                halo_recv.at[level, side],
                me - 1 if up else me + 1,
            )

        def send_halo(level):
            @pl.when(has_low)
            def _():
                halo_copy(level, True).start()

            @pl.when(has_high)
            def _():
                halo_copy(level, False).start()

        def await_halo(level):
            @pl.when(has_low)
            def _():
                halo_copy(level, False).wait_recv()

            @pl.when(has_high)
            def _():
                halo_copy(level, True).wait_recv()

        count = len(steps)
        for step in range(count + PAIR_LAG):
            if step < count:
                compute(step)
                if step == 0:
                    pl.semaphore_wait(barrier, n - 1)
                    send_halo(0)
                core_copy(step).start()
            if CORE_LAG <= step < count + CORE_LAG:
                last = step - CORE_LAG
                block, half = steps[last]
                core_copy(last).wait_recv()
                other = 1 - pair
                part[block, half, core, other, 0:third] = (
                    part[block, half, core, other, 0:third] + core_in[block, half, other, 0:third]
                )
                pair_half_out[block, half] = (
                    part[block, half, core, other, third:lines]
                    + core_in[block, half, other, third:lines]
                ).astype(jnp.bfloat16)
                for copy in pair_copies(last):
                    copy.start()
                part[block, half, core, pair] = (
                    part[block, half, core, pair] + core_in[block, half, pair]
                )
            if step >= PAIR_LAG:
                last = step - PAIR_LAG
                block, half = steps[last]
                for copy in pair_copies(last):
                    copy.wait_recv()
                part[block, half, core, pair, 0:third] = (
                    part[block, half, core, pair, 0:third] + pair_in[block, half]
                )
                rest = part[block, half, core, pair, third:lines] + pair_half_in[
                    block, half
                ].astype(jnp.float32)
                part[block, half, core, pair, third:lines] = rest
                block_half_out[block, half] = rest[third:].astype(jnp.bfloat16)

                @pl.when(zone != block)
                def _(last=last):
                    for copy in block_copies(last, zone):
                        copy.start()

        for half in range(HALVES):
            step = steps.index((0, half))
            total = part[zone, half, core, pair, 0 : 2 * third]
            small = part[zone, half, core, pair, 2 * third : lines]
            for shift in range(1, blocks):
                source = lax.rem(zone + shift, blocks)
                for copy in block_copies(step, source):
                    copy.wait_recv()
                total = total + block_in[source, half]
                small = small + block_half_in[source, half].astype(jnp.float32)
            sums[0 : 2 * third, half * width : (half + 1) * width] = total
            sums[2 * third : lines, half * width : (half + 1) * width] = small

        def lines_of(spot, length=1):
            return pl.ds(rows_here * spot, rows_here * length)

        n00, n01, n02, _, n12, n22 = (lines_of(spot) for spot in normal_at)
        sums[n22] = sums[n22] + 2.0 * geo_centre * sums[n02] + geo_centre**2 * sums[n00]
        sums[n12] = sums[n12] + geo_centre * sums[n01]
        sums[n02] = sums[n02] + geo_centre * sums[n00]
        geo_lines = lines_of(signal_at[2], bands)
        sums[geo_lines] = sums[geo_lines] + geo_centre * sums[lines_of(signal_at[0], bands)]

        lane = lax.broadcasted_iota(jnp.int32, (8, cols), 1)
        first_col = lane == 0
        last_col = lane == cols - 1
        edge_cols = first_col.astype(jnp.float32) + last_col.astype(jnp.float32)

        def normal_entry(row, entry):
            line = rows_here * normal_at[entry] + row
            return jnp.broadcast_to(sums[line : line + 1, :], (8, cols))

        pick = ((0, 1, 2), (1, 3, 4), (2, 4, 5))

        def apply(level):
            result = []
            for row in range(rows_here):
                position = me * rows_here + row
                inside = (
                    4.0
                    - (position == 0).astype(jnp.float32)
                    - (position == total_rows - 1).astype(jnp.float32)
                )
                own = prior_pull + smooth_pull * (inside - edge_cols)
                line = []
                for kern in range(3):
                    here = field[level, row, kern]
                    before = jnp.where(first_col, 0.0, pltpu.roll(here, 1, 1))
                    after = jnp.where(last_col, 0.0, pltpu.roll(here, cols - 1, 1))
                    beside = before + after
                    if row > 0:
                        beside = beside + field[level, row - 1, kern]
                    if row < rows_here - 1:
                        beside = beside + field[level, row + 1, kern]
                    image = own * here - smooth_pull * beside
                    for other in range(3):
                        image = image + normal_entry(row, pick[kern][other]) * field[level, row, other]
                    line.append(image)
                result.append(line)
            await_halo(level)
            for kern in range(3):
                result[0][kern] = result[0][kern] - smooth_pull * halo[level, 0, kern]
                result[-1][kern] = result[-1][kern] - smooth_pull * halo[level, 1, kern]
            return result

        cells = [(row, kern) for row in range(rows_here) for kern in range(3)]
        image = apply(0)
        for row, kern in cells:
            for band in range(bands):
                line = rows_here * (signal_at[kern] + band) + row
                field[1, row, kern, band : band + 1, :] = sums[line : line + 1, :]
        for row, kern in cells:
            field[1, row, kern] = (
                field[1, row, kern] + prior_pull * field[0, row, kern] - image[row][kern]
            )
        send_halo(1)

        def inner(left, right):
            total = None
            for row, kern in cells:
                term = left(row, kern) * right(row, kern)
                total = term if total is None else total + term
            return jnp.sum(jnp.sum(total, axis=0, keepdims=True), axis=1, keepdims=True)

        def stored(level):
            return lambda row, kern: field[level, row, kern]

        moments = [inner(stored(1), stored(1))]
        for level in (1, 2):
            image = apply(level)
            for row, kern in cells:
                field[level + 1, row, kern] = image[row][kern] - basis_shift * field[level, row, kern]
            send_halo(level + 1)
            moments.append(inner(stored(level), stored(level + 1)))
            moments.append(inner(stored(level + 1), stored(level + 1)))
        image = apply(3)
        moments.append(
            inner(
                stored(3),
                lambda row, kern: image[row][kern] - basis_shift * field[3, row, kern],
            )
        )
        small_lane = lax.broadcasted_iota(jnp.int32, (1, LANES), 1)
        packed = jnp.zeros((1, LANES), jnp.float32)
        for index, value in enumerate(moments):
            packed = jnp.where(small_lane == index, value, packed)
        moment_out[...] = packed

        def moment_copy(target, source):
            return remote(
                moment_out,
                moment_in.at[source],
                moment_send.at[target],
                moment_recv.at[source],
                target,
            )

        for step in range(1, n):
            moment_copy(lax.rem(me + step, n), me).start()
        gathered = packed
        for step in range(1, n):
            source = lax.rem(me + step, n)
            moment_copy(source, source).wait_recv()
            gathered = gathered + moment_in[source]
        m = [
            jnp.sum(jnp.where(small_lane == index, gathered, 0.0), axis=1, keepdims=True)
            for index in range(len(moments))
        ]

        def form(coefs, with_operator):
            total = 0.0
            for i, a in enumerate(coefs):
                for j, b in enumerate(coefs):
                    moment = m[i + j]
                    if with_operator:
                        moment = m[i + j + 1] + basis_shift * moment
                    total = total + a * b * moment
            return total

        one = jnp.ones((1, 1), jnp.float32)
        residual = [one]
        direction = [one]
        answer = [0.0, 0.0, 0.0]
        rho = m[0]
        for iteration in range(3):
            alpha = rho / form(direction, True)
            answer = [
                a + (alpha * direction[i] if i < len(direction) else 0.0)
                for i, a in enumerate(answer)
            ]
            if iteration < 2:
                image = [basis_shift * d for d in direction] + [0.0]
                for i, d in enumerate(direction):
                    image[i + 1] = image[i + 1] + d
                residual = [
                    (residual[i] if i < len(residual) else 0.0) - alpha * image[i]
                    for i in range(len(image))
                ]
                rho_next = form(residual, False)
                ratio = rho_next / rho
                direction = [
                    residual[i] + (ratio * direction[i] if i < len(direction) else 0.0)
                    for i in range(len(residual))
                ]
                rho = rho_next
        for row, kern in cells:
            value = field[0, row, kern]
            for level in range(3):
                value = value + answer[level] * field[level + 1, row, kern]
            for band in range(bands):
                line = 3 * band + kern
                out_ref[line, row : row + 1, :] = value[band : band + 1]

        for step in range(count):
            core_copy(step).wait_send()
            for copy in pair_copies(step):
                copy.wait_send()

            @pl.when(zone != steps[step][0])
            def _(step=step):
                for copy in block_copies(step, zone):
                    copy.wait_send()

        for level in range(4):

            @pl.when(has_low)
            def _(level=level):
                halo_copy(level, True).wait_send()

            @pl.when(has_high)
            def _(level=level):
                halo_copy(level, False).wait_send()

        for step in range(1, n):
            moment_copy(lax.rem(me + step, n), me).wait_send()

    count = len(steps)
    f32 = jnp.float32
    dma = pltpu.SemaphoreType.DMA
    scratch = [
        pltpu.VMEM((blocks, dates, bands, tall, cols), jnp.bfloat16),
        pltpu.VMEM((blocks, dates, tall, cols), jnp.int32),
        pltpu.VMEM((blocks, dates, 3, tall, cols), jnp.int32),
        pltpu.VMEM((blocks, HALVES, 2, 2, lines, width), f32),
        pltpu.VMEM((blocks, HALVES, 2, lines, width), f32),
        pltpu.VMEM((blocks, HALVES, lines // 3, width), f32),
        pltpu.VMEM((blocks, HALVES, 2 * lines // 3, width), f32),
        pltpu.VMEM((lines, cols), f32),
        pltpu.VMEM((4, rows_here, 3, 8, cols), f32),
        pltpu.VMEM((4, 2, 3, 8, cols), f32),
        pltpu.VMEM((1, LANES), f32),
        pltpu.VMEM((n, 1, LANES), f32),
        pltpu.VMEM((blocks, HALVES, 2 * lines // 3, width), jnp.bfloat16),
        pltpu.VMEM((blocks, HALVES, 2 * lines // 3, width), jnp.bfloat16),
        pltpu.VMEM((blocks, HALVES, lines // 3, width), jnp.bfloat16),
        pltpu.VMEM((blocks, HALVES, lines // 3, width), jnp.bfloat16),
        dma((count,)),
        dma((count,)),
        dma((count,)),
        dma((blocks, HALVES)),
        dma((blocks, 3)),
        dma((count,)),
        dma((count,)),
        dma((count,)),
        dma((count,)),
        dma((count,)),
        dma((blocks, HALVES)),
        dma((4, 2)),
        dma((4, 2)),
        dma((n,)),
        dma((n,)),
    ]
    return kernel, scratch


def solution(mesh):
    n = mesh.shape["rows"]

    def on_device(reflect, clear_conf, sun_view, sensor_id, band_gain, sensor_weight, prior):
        dates, bands, total_rows, cols = reflect.shape
        kernel, scratch = make_kernel(n, dates, bands, total_rows, cols, prior.shape[0])
        smem = pl.BlockSpec(memory_space=pltpu.SMEM)
        vmem = pl.BlockSpec(memory_space=pltpu.VMEM)
        hbm = pl.BlockSpec(memory_space=pl.ANY)
        stored = prior.transpose(1, 0, 2)
        solved = pl.pallas_call(
            kernel,
            out_shape=jax.ShapeDtypeStruct(stored.shape, jnp.float32),
            in_specs=[smem, smem, smem, vmem, hbm, hbm, hbm],
            out_specs=vmem,
            scratch_shapes=scratch,
            compiler_params=pltpu.CompilerParams(
                collective_id=0, has_side_effects=True, vmem_limit_bytes=60 * 1024 * 1024
            ),
        )(sensor_id, band_gain, sensor_weight, stored, reflect, clear_conf, sun_view)
        return solved.transpose(1, 0, 2)

    return jax.shard_map(
        on_device,
        mesh=mesh,
        in_specs=(
            P("rows", None, None, "tiles"),
            P("rows", None, "tiles"),
            P("rows", None, None, "tiles"),
            P(),
            P(),
            P(),
            P("rows", None, "tiles"),
        ),
        out_specs=P("rows", None, "tiles"),
        check_vma=False,
    )
```
